32 devices in a mesh: rep: 2 (over y), cache: 8 (over z, x), head: 2 (over core).
Axes of the slice: x: 2, y: 2, z: 4, core: 2. Of those that a mesh axis runs over, the one named last changes fastest.
Arguments:
- reception_vectors: bfloat16 [16, 128, 4096], P(('rep', 'cache'), None, 'head'), parts along dimension 0, may hold values from -6 to 6
- address_vectors: bfloat16 [16, 128, 4096], P(('rep', 'cache'), None, 'head'), parts along dimension 0, may hold values from -0.75 to 0.75
- payload_vectors: bfloat16 [16, 128, 4096], P(('rep', 'cache'), None, 'head'), parts along dimension 0, may hold values from -6 to 6
- emission_switch_preact: bfloat16 [16, 128, 4096], P(('rep', 'cache'), None, 'head'), parts along dimension 0, may hold values from -6 to 6
- fading_rates: bfloat16 [16, 128, 4096], P(('rep', 'cache'), None, 'head'), parts along dimension 0, may hold values from 0 to 1, as said below
- present_extra_coefficient: float32 [64, 64], P('head'), may hold values from -5 to 5
- saved_memory_matrix: bfloat16 [64, 64, 64, 64], P(('rep', 'cache'), 'head'), parts along dimension 0, may hold values from -6 to 6
- layernorm_scale: float32 [4096], P('head'), may hold values from 0.1 to 1.9
- layernorm_shift: float32 [4096], P('head'), may hold values from -3 to 3
- stored_memory_locator: int32 [16, 2], P(('rep', 'cache')), parts along dimension 0, may hold values from 0 to 7, as said below
Outputs:
- mixed: bfloat16 [16, 128, 4096], P(('rep', 'cache'), None, 'head'), parts along dimension 0
- final_states: float32 [16, 64, 64, 64], P(('rep', 'cache'), 'head'), parts along dimension 0
The draws below stay inside these ranges and needn't reach their ends.
There are 2 independent parts, one for each index of `rep`. The reference program is written for one: setup_inputs(seed, part) draws one part's arguments, and reference() takes and returns one part's arrays. A program takes and returns all parts, laid end to end along the dimension named above; an argument that names none is the same for every part. Nothing has to cross between parts.
Inputs may be any that keep to these rules, and one draw needn't show every extreme that they name: `fading_rates`: positive decay rates. `stored_memory_locator`: the requests that name one cache index name at most 2 distinct slots of it, and in every draw some cache index has exactly 2 named slots.
All inputs are finite; a program needn't handle non-finite values.
Results may differ from the reference program's by a relative error of at most 0.001.
Values may be sent and summed in bfloat16 or wider, within the bound.
No kernel may reach another device: no remote copies, remote signals or barrier semaphores. Data moves between devices by JAX's collectives and lax.ppermute only.
A program may use at most 64 MiB of HBM per device.

```python
import jax
import jax.numpy as jnp
from jax import lax

ATTENTION_GROUPS = 64
GROUP_DIMENSION = 64
D = 4096
SUFFIX_LENGTH = 128
GROUP = 64
SLOTS = 4
HITS = 2
REQUEST_TOTAL = 8
N_CACHE = 8


def draw_fading_rates(key, part):
    base = jax.random.fold_in(key, 101)
    key_rows = jax.random.split(base, 8)
    head_rate = jnp.exp(jax.random.uniform(key_rows[0], (ATTENTION_GROUPS,), minval=jnp.log(0.5 / SUFFIX_LENGTH), maxval=jnp.log(0.05)))
    channel = jax.random.uniform(key_rows[3], (ATTENTION_GROUPS, GROUP_DIMENSION), minval=0.7, maxval=1.3)
    request_factor = jnp.exp(jax.random.uniform(key_rows[4], (REQUEST_TOTAL, 1, 1, 1), minval=jnp.log(0.6), maxval=jnp.log(1.5)))
    token_factor = jax.random.uniform(key_rows[5], (REQUEST_TOTAL, SUFFIX_LENGTH, ATTENTION_GROUPS, GROUP_DIMENSION), minval=0.5, maxval=1.5)
    request_tokens = jax.random.randint(key_rows[6], (REQUEST_TOTAL, SUFFIX_LENGTH, ATTENTION_GROUPS, 1), 0, 32) == 0
    decay_strength = jax.random.uniform(key_rows[7], (REQUEST_TOTAL, SUFFIX_LENGTH, ATTENTION_GROUPS, 1), minval=0.22, maxval=0.7)
    decay_factor = (head_rate[:, None] * channel)[None, None] * request_factor * token_factor
    decay_factor = decay_factor + jnp.where(request_tokens, decay_strength, 0.0)
    return decay_factor.reshape(REQUEST_TOTAL, SUFFIX_LENGTH, ATTENTION_GROUPS * GROUP_DIMENSION).astype(jnp.bfloat16)


def draw_stored_memory_locator(key, part):
    base = jax.random.fold_in(key, 202)
    key_rows = jax.random.split(base, 7)
    hot_owners = jax.random.randint(key_rows[0], (4,), 0, REQUEST_TOTAL)
    hot_pick = jax.random.randint(key_rows[1], (REQUEST_TOTAL,), 0, 4)
    spread_owner = jax.random.randint(key_rows[2], (REQUEST_TOTAL,), 0, REQUEST_TOTAL)
    hot_index = jax.random.randint(key_rows[3], (REQUEST_TOTAL,), 0, 4)
    owner = jnp.where(hot_pick == 0, hot_owners[hot_index], spread_owner)
    chosen = jax.random.randint(key_rows[4], (REQUEST_TOTAL,), 0, HITS)
    orders = jax.vmap(lambda one_key: jax.random.permutation(one_key, SLOTS))(jax.random.split(key_rows[5], REQUEST_TOTAL))
    forced = jax.random.permutation(key_rows[6], REQUEST_TOTAL)[:HITS]
    owner = owner.at[forced].set(hot_owners[0])
    chosen = chosen.at[forced].set(jnp.arange(HITS, dtype=jnp.int32))
    slot = orders[owner, chosen]
    return jnp.stack([owner, slot], axis=1).astype(jnp.int32)


def steps_of(own_key, dims, cuts, smallest, largest):
    factor_of, own = 1.0, jax.random.fold_in(own_key, 6)
    for position, blocks in cuts:
        draws = jnp.exp(jax.random.uniform(jax.random.fold_in(own, position), (blocks,), jnp.float32, smallest / len(cuts), largest / len(cuts)))
        factor_of = factor_of * jnp.repeat(draws, dims[position] // blocks).reshape([-1 if axis == position else 1 for axis in range(len(dims))])
    return factor_of


def scatter_about(stream_key, dims, scale, bound, pieces=(), kind=jnp.bfloat16):
    entries = scale * jax.random.normal(stream_key, dims, jnp.float32)
    if pieces:
        entries = entries * steps_of(stream_key, dims, pieces, -0.22, 0.18)
    return jnp.clip(entries, -bound, bound).astype(kind)


def setup_inputs(seed: int = 0, part: int = 0) -> dict:
    seeds = jax.random.split(jax.random.key(seed), 11)
    part_keys = jax.random.split(jax.random.fold_in(seeds[10], part), 11)
    return {
        "reception_vectors": scatter_about(part_keys[0], (REQUEST_TOTAL, SUFFIX_LENGTH, D), 1.0, 6.0, ((0, 8), (2, 2))),
        "address_vectors": scatter_about(part_keys[1], (REQUEST_TOTAL, SUFFIX_LENGTH, D), 0.125, 0.75, ((0, 8), (2, 2))),
        "payload_vectors": scatter_about(part_keys[2], (REQUEST_TOTAL, SUFFIX_LENGTH, D), 1.0, 6.0, ((0, 8), (2, 2))),
        "emission_switch_preact": scatter_about(part_keys[3], (REQUEST_TOTAL, SUFFIX_LENGTH, D), 1.0, 6.0, ((0, 8), (2, 2))),
        "fading_rates": draw_fading_rates(jax.random.fold_in(jax.random.fold_in(seeds[10], part), 71), part),
        "present_extra_coefficient": scatter_about(seeds[5], (ATTENTION_GROUPS, GROUP_DIMENSION), 1.0, 5.0, ((0, 2),), jnp.float32),
        "saved_memory_matrix": scatter_about(part_keys[6], (N_CACHE * SLOTS, ATTENTION_GROUPS, GROUP_DIMENSION, GROUP_DIMENSION), 1.0, 6.0, ((0, 8), (1, 2))),
        "layernorm_scale": jnp.clip(1.0 + 0.18 * jax.random.normal(seeds[7], (D,), jnp.float32), 0.1, 1.9),
        "layernorm_shift": scatter_about(seeds[8], (D,), 0.5, 3.0, ((0, 2),), jnp.float32),
        "stored_memory_locator": draw_stored_memory_locator(jax.random.fold_in(jax.random.fold_in(seeds[10], part), 71), part),
    }


def linear_attention_scan(reception_vectors, address_vectors, payload_vectors, fading_rates, present_extra_coefficient, initial_memory):
    length, head_count, group_features = reception_vectors.shape
    blocks = length // GROUP

    def arrange(values):
        return values.reshape(blocks, GROUP, head_count, group_features).transpose(0, 2, 1, 3)
    positions = jnp.arange(GROUP)
    strict_lower = positions[:, None] > positions[None, :]
    identity = jnp.eye(GROUP, dtype=jnp.float32)
    highest = lax.Precision.HIGHEST

    def advance(carry_state, block_data):
        reception_portion, address_portion, value_part, forget_part = block_data
        decay_sum = jnp.cumsum(-forget_part, axis=1)
        before = decay_sum + forget_part
        queries = reception_portion * jnp.exp(before)
        scaled_keys = address_portion * jnp.exp(-decay_sum)
        scores = jnp.einsum('htc,hjc->htj', queries, scaled_keys, precision=highest)
        diagonal_term = lax.optimization_barrier(jnp.sum(reception_portion * present_extra_coefficient[:, None, :] * address_portion, axis=2))
        scores = jnp.where(strict_lower[None], scores, 0.0) + diagonal_term[:, :, None] * identity[None]
        emitted_entries = jnp.einsum('htj,hjv->htv', scores, value_part, precision=highest)
        emitted_entries = emitted_entries + jnp.einsum('htc,hcv->htv', queries, carry_state, precision=highest)
        group_total = decay_sum[:, -1:, :]
        carried = address_portion * jnp.exp(group_total - decay_sum)
        carry_state = jnp.exp(group_total[:, 0, :])[:, :, None] * carry_state + jnp.einsum('hjc,hjv->hcv', carried, value_part, precision=highest)
        return (carry_state, emitted_entries)
    terminal_memory, emitted_entries = lax.scan(advance, initial_memory, (arrange(reception_vectors), arrange(address_vectors), arrange(payload_vectors), arrange(fading_rates)))
    emitted_entries = emitted_entries.transpose(0, 2, 1, 3).reshape(length, head_count, group_features)
    return (emitted_entries, terminal_memory)

def finish(emitted_entries, emission_switch_preact, layernorm_scale, layernorm_shift):
    head_mean = lax.optimization_barrier(jnp.mean(emitted_entries, axis=2, keepdims=True))
    centered = emitted_entries - head_mean
    head_var = lax.optimization_barrier(jnp.mean(centered * centered, axis=2, keepdims=True))
    normed = (centered * lax.rsqrt(head_var + 1e-05)).reshape(emitted_entries.shape[0], -1)
    gate_float = emission_switch_preact.astype(jnp.float32)
    return ((normed * layernorm_scale + layernorm_shift) * jax.nn.silu(gate_float)).astype(jnp.bfloat16)

def reference(reception_vectors, address_vectors, payload_vectors, emission_switch_preact, fading_rates, present_extra_coefficient, saved_memory_matrix, layernorm_scale, layernorm_shift, stored_memory_locator):
    requests = reception_vectors.shape[0]
    head_shape = (reception_vectors.shape[1], ATTENTION_GROUPS, GROUP_DIMENSION)

    def one_request(request):
        cache_row = (stored_memory_locator[request, 0] * SLOTS + stored_memory_locator[request, 1]).astype(jnp.int32)
        initial_memory = lax.dynamic_index_in_dim(saved_memory_matrix, cache_row, 0, keepdims=False).astype(jnp.float32)

        def divide_among_groups(values):
            return values[request].astype(jnp.float32).reshape(head_shape)
        emitted_entries, terminal_memory = linear_attention_scan(divide_among_groups(reception_vectors), divide_among_groups(address_vectors), divide_among_groups(payload_vectors), divide_among_groups(fading_rates), present_extra_coefficient, initial_memory)
        return (finish(emitted_entries, emission_switch_preact[request], layernorm_scale, layernorm_shift), terminal_memory)
    mixed, final_states = lax.map(one_request, jnp.arange(requests, dtype=jnp.int32))
    return (mixed, final_states)
```

```python
import functools

import jax
import jax.numpy as jnp
from jax import lax
from jax.experimental import pallas as pl
from jax.experimental.pallas import tpu as pltpu
from jax.sharding import PartitionSpec as P

GROUP = 64
HITS = 2
F32 = jnp.float32
BF16 = jnp.bfloat16


def split(x):
    hi = x.astype(BF16)
    lo = (x - hi.astype(F32)).astype(BF16)
    return hi, lo


def mm(a, b):
    return lax.dot_general(a, b, (((1,), (0,)), ((), ())), preferred_element_type=F32)


def mm_nt(a, b):
    return lax.dot_general(a, b, (((1,), (1,)), ((), ())), preferred_element_type=F32)


def mm_tn(a, b):
    return lax.dot_general(a, b, (((0,), (0,)), ((), ())), preferred_element_type=F32)


def lane_of(rows, lanes):
    return lax.broadcasted_iota(jnp.int32, (rows, lanes), 1)


def diag_pair(x, first):
    zero = jnp.zeros_like(x)
    return jnp.concatenate([jnp.where(first, x, zero), jnp.where(first, zero, x)], axis=0)


def pack_kernel(table_ref, saved_ref, out_ref, held, packed, in_sem, out_sem, *, parts):
    devices = out_ref.shape[0]
    rows = out_ref.shape[2]
    slots, heads, chans, _ = saved_ref.shape
    me = lax.axis_index("cache")

    def scan(i, used):
        bit = lax.shift_left(jnp.int32(1), table_ref[i, 1])
        return used | jnp.where(table_ref[i, 0] == me, bit, 0)

    used = lax.fori_loop(0, devices, scan, jnp.int32(0), unroll=min(8, devices))
    first = jnp.int32(0)
    second = jnp.int32(0)
    for s in reversed(range(slots)):
        has = (lax.shift_right_logical(used, s) & 1) == 1
        second = jnp.where(has, first, second)
        first = jnp.where(has, s, first)
    chosen = (first, second)
    step = heads // parts

    def load(part, hit):
        return pltpu.make_async_copy(
            saved_ref.at[chosen[hit], pl.ds(part * step, step)],
            held.at[hit, pl.ds(part * step, step)],
            in_sem.at[part, hit],
        )

    span = devices // parts

    def store(part, hit):
        return pltpu.make_async_copy(
            packed.at[pl.ds(part * span, span), hit],
            out_ref.at[pl.ds(part * span, span), hit],
            out_sem.at[part, hit],
        )

    for part in range(parts):
        for hit in range(HITS):
            load(part, hit).start()
    for part in range(parts):
        for hit in range(HITS):
            load(part, hit).wait()
            even = held[hit, pl.ds(part * step, step // 2, 2)]
            odd = held[hit, pl.ds(part * step + 1, step // 2, 2)]
            both = jnp.concatenate([even, odd], axis=-1)
            packed[part * span : (part + 1) * span, hit] = both.reshape(span, rows, 2 * chans)
            store(part, hit).start()
    for part in range(parts):
        for hit in range(HITS):
            store(part, hit).wait()


def pick_kernel(wanted_ref, arrived_ref, out_ref, held, in_sem, out_sem):
    devices = out_ref.shape[0]

    def load(d):
        w = wanted_ref[d]
        return pltpu.make_async_copy(
            arrived_ref.at[w // HITS, w % HITS], held.at[d], in_sem.at[d]
        )

    def store(d):
        return pltpu.make_async_copy(held.at[d], out_ref.at[d], out_sem.at[d])

    def each(f):
        lax.fori_loop(0, devices, lambda d, c: (f(d), c)[1], 0, unroll=min(8, devices))

    def turn(d):
        load(d).wait()
        store(d).start()

    each(lambda d: load(d).start())
    each(turn)
    each(lambda d: store(d).wait())


def inner_kernel(r_ref, k_ref, v_ref, f_ref, u_ref, o_ref, q_ref, part_ref, dec_ref):
    length, lanes = r_ref.shape
    wide = 2 * GROUP
    first = lane_of(GROUP, wide) < GROUP
    position = lane_of(GROUP, wide) % GROUP
    token = lax.broadcasted_iota(jnp.int32, (GROUP, wide), 0)
    lower = token > position
    row = lax.broadcasted_iota(jnp.int32, (length, length), 0)
    col = lax.broadcasted_iota(jnp.int32, (length, length), 1)
    triangle = ((row >= col) & (row // GROUP == col // GROUP)).astype(F32).astype(BF16)
    w_row = lax.broadcasted_iota(jnp.int32, (wide, wide), 0)
    w_col = lax.broadcasted_iota(jnp.int32, (wide, wide), 1)
    head_ones = (w_row // GROUP == w_col // GROUP).astype(F32).astype(BF16)
    ones = jnp.ones((length, wide), BF16)
    chunks = length // GROUP

    for pair in range(lanes // wide):
        at = slice(pair * wide, (pair + 1) * wide)
        f = f_ref[:, at]
        r = r_ref[:, at].astype(F32)
        k = k_ref[:, at].astype(F32)
        v = v_ref[:, at]
        cum = mm(triangle, f)
        q = r * jnp.exp(f.astype(F32) - cum)
        ks = k * jnp.exp(cum)
        x_hi, x_lo = split(r * u_ref[:, at] * k)
        bonus = mm(x_hi, head_ones) + mm(x_lo, head_ones)
        total = mm_tn(f, ones)
        dec_ref[pair] = jnp.exp(-jnp.where(first, total[:GROUP], total[GROUP:]))
        decays = [jnp.exp(-cum[(c + 1) * GROUP - 1 : (c + 1) * GROUP]) for c in range(chunks)]
        state = None
        start = None
        weights = []
        for c in range(chunks):
            rows = slice(c * GROUP, (c + 1) * GROUP)
            q_c = q[rows]
            q_hi, q_lo = split(q_c)
            k_hi, k_lo = split(ks[rows])
            v_c = v[rows]
            kd_hi = diag_pair(k_hi, first)
            kd_lo = diag_pair(k_lo, first)
            scores = mm_nt(q_hi, kd_hi) + mm_nt(q_lo, kd_hi) + mm_nt(q_hi, kd_lo)
            s_hi, s_lo = split(jnp.where(lower, scores, 0.0))
            vd = diag_pair(v_c, first)
            out = bonus[rows] * v_c.astype(F32) + mm(s_hi, vd) + mm(s_lo, vd)
            if c:
                p_hi, p_lo = split(state)
                pd_hi = diag_pair(p_hi, first)
                pd_lo = diag_pair(p_lo, first)
                out = out + mm(q_hi, pd_hi) + mm(q_lo, pd_hi) + mm(q_hi, pd_lo)
                q_c = q_c * start
                q_hi, q_lo = split(q_c)
            o_ref[rows, at] = out
            q_ref[rows, 2 * pair * wide : (2 * pair + 1) * wide] = q_hi
            q_ref[rows, (2 * pair + 1) * wide : (2 * pair + 2) * wide] = q_lo
            carried = ks[rows] * decays[c]
            if c < chunks - 1:
                c_hi, c_lo = split(carried)
                full = mm_tn(c_hi, v_c) + mm_tn(c_lo, v_c)
                grown = jnp.where(first, full[:GROUP], full[GROUP:])
                if state is not None:
                    total_c = mm_tn(f[rows], ones[rows])
                    keep = jnp.exp(-jnp.where(first, total_c[:GROUP], total_c[GROUP:]))
                    grown = grown + keep * state
                state = grown
                start = decays[c] if start is None else start * decays[c]
            for later in range(c + 1, chunks):
                carried = carried * decays[later]
            weights.append(carried)
        c_hi, c_lo = split(jnp.concatenate(weights, axis=0))
        full = mm_tn(c_hi, v) + mm_tn(c_lo, v)
        part_ref[pair] = jnp.where(first, full[:GROUP], full[GROUP:])


def outer_kernel(s_ref, o_ref, q_ref, part_ref, dec_ref, g_ref, gain_ref, bias_ref, mixed_ref, final_ref):
    length, lanes = o_ref.shape
    wide = 2 * GROUP
    first = lane_of(GROUP, wide) < GROUP
    w_row = lax.broadcasted_iota(jnp.int32, (wide, wide), 0)
    w_col = lax.broadcasted_iota(jnp.int32, (wide, wide), 1)
    mean_w = jnp.where(w_row // GROUP == w_col // GROUP, 1.0 / GROUP, 0.0).astype(BF16)
    for pair in range(lanes // wide):
        at = slice(pair * wide, (pair + 1) * wide)
        s = s_ref[pair]
        sd = diag_pair(s, first)
        q_hi = q_ref[:, 2 * pair * wide : (2 * pair + 1) * wide]
        q_lo = q_ref[:, (2 * pair + 1) * wide : (2 * pair + 2) * wide]
        out = o_ref[:, at] + mm(q_hi, sd) + mm(q_lo, sd)
        hi, lo = split(out)
        centered = out - (mm(hi, mean_w) + mm(lo, mean_w))
        hi, lo = split(centered * centered)
        var = mm(hi, mean_w) + mm(lo, mean_w)
        normed = centered * lax.rsqrt(var + 1e-05)
        g = g_ref[:, at].astype(F32)
        gate = g / (1.0 + jnp.exp(-g))
        mixed_ref[:, at] = ((normed * gain_ref[:, at] + bias_ref[:, at]) * gate).astype(BF16)
        last = dec_ref[pair] * s.astype(F32) + part_ref[pair]
        final_ref[2 * pair] = last[:, :GROUP]
        final_ref[2 * pair + 1] = last[:, GROUP:]


def body(
    reception_vectors,
    address_vectors,
    payload_vectors,
    emission_switch_preact,
    fading_rates,
    present_extra_coefficient,
    saved_memory_matrix,
    layernorm_scale,
    layernorm_shift,
    stored_memory_locator,
):
    devices = lax.axis_size("cache")
    heads, chans = present_extra_coefficient.shape
    slots = saved_memory_matrix.shape[0]
    length, lanes = reception_vectors.shape[1:]
    pairs = heads // 2
    wide = 2 * chans
    rows = pairs * chans // devices
    parts = min(4, devices)

    table = lax.all_to_all(
        jnp.broadcast_to(stored_memory_locator, (devices, 2)), "cache", 0, 0, tiled=True
    )

    anywhere = pl.BlockSpec(memory_space=pl.ANY)
    scalars = pl.BlockSpec(memory_space=pltpu.SMEM)
    outgoing = pl.pallas_call(
        functools.partial(pack_kernel, parts=parts),
        name="pack",
        out_shape=jax.ShapeDtypeStruct((devices, HITS, rows, wide), BF16),
        in_specs=[scalars, anywhere],
        out_specs=anywhere,
        scratch_shapes=[
            pltpu.VMEM((HITS, heads, chans, chans), BF16),
            pltpu.VMEM((devices, HITS, rows, wide), BF16),
            pltpu.SemaphoreType.DMA((parts, HITS)),
            pltpu.SemaphoreType.DMA((parts, HITS)),
        ],
        cost_estimate=pl.CostEstimate(flops=0, transcendentals=0, bytes_accessed=3 << 20),
    )(table, saved_memory_matrix)
    arrived = lax.all_to_all(outgoing, "cache", 0, 0, tiled=True)

    owner = table[:, 0]
    slot = table[:, 1]
    same = owner[:, None] == owner[None, :]
    ids = jnp.arange(slots, dtype=jnp.int32)
    named = jnp.any(same[:, :, None] & (slot[None, :, None] == ids), axis=1)
    rank = jnp.sum((named & (ids[None, :] < slot[:, None])).astype(jnp.int32), axis=1)
    wanted = owner * HITS + rank

    steps = 4
    block = lanes // steps
    per = pairs // steps
    tokens = pl.BlockSpec((length, block), lambda i: (0, i))
    row_of = pl.BlockSpec((1, block), lambda i: (0, i))
    states = pl.BlockSpec((per, chans, wide), lambda i: (i, 0, 0))
    doubled = pl.BlockSpec((length, 2 * block), lambda i: (0, i))
    inner, queries, partial, decay = pl.pallas_call(
        inner_kernel,
        name="inner",
        grid=(steps,),
        out_shape=(
            jax.ShapeDtypeStruct((length, lanes), F32),
            jax.ShapeDtypeStruct((length, 2 * lanes), BF16),
            jax.ShapeDtypeStruct((pairs, chans, wide), F32),
            jax.ShapeDtypeStruct((pairs, chans, wide), F32),
        ),
        in_specs=[tokens, tokens, tokens, tokens, row_of],
        out_specs=(tokens, doubled, states, states),
        cost_estimate=pl.CostEstimate(flops=1 << 32, transcendentals=1 << 20, bytes_accessed=16 << 20),
    )(
        reception_vectors[0],
        address_vectors[0],
        payload_vectors[0],
        fading_rates[0],
        present_extra_coefficient.reshape(1, lanes),
    )

    selected = pl.pallas_call(
        pick_kernel,
        name="pick",
        out_shape=jax.ShapeDtypeStruct((devices, rows, wide), BF16),
        in_specs=[scalars, anywhere],
        out_specs=anywhere,
        scratch_shapes=[
            pltpu.VMEM((devices, rows, wide), BF16),
            pltpu.SemaphoreType.DMA((devices,)),
            pltpu.SemaphoreType.DMA((devices,)),
        ],
        cost_estimate=pl.CostEstimate(flops=0, transcendentals=0, bytes_accessed=1 << 20),
    )(wanted, arrived)
    delivered = lax.all_to_all(selected, "cache", 0, 0, tiled=True)

    mixed, final = pl.pallas_call(
        outer_kernel,
        name="outer",
        grid=(steps,),
        out_shape=(
            jax.ShapeDtypeStruct((length, lanes), BF16),
            jax.ShapeDtypeStruct((heads, chans, chans), F32),
        ),
        in_specs=[states, tokens, doubled, states, states, tokens, row_of, row_of],
        out_specs=(tokens, pl.BlockSpec((2 * per, chans, chans), lambda i: (i, 0, 0))),
        cost_estimate=pl.CostEstimate(flops=1 << 30, transcendentals=1 << 20, bytes_accessed=8 << 20),
    )(
        delivered.reshape(pairs, chans, wide),
        inner,
        queries,
        partial,
        decay,
        emission_switch_preact[0],
        layernorm_scale.reshape(1, lanes),
        layernorm_shift.reshape(1, lanes),
    )
    return (mixed[None], final[None])


def solution(mesh):
    in_specs = (
        P(("rep", "cache"), None, "head"),
        P(("rep", "cache"), None, "head"),
        P(("rep", "cache"), None, "head"),
        P(("rep", "cache"), None, "head"),
        P(("rep", "cache"), None, "head"),
        P("head", None),
        P(("rep", "cache"), "head", None, None),
        P("head"),
        P("head"),
        P(("rep", "cache"), None),
    )
    out_specs = (P(("rep", "cache"), None, "head"), P(("rep", "cache"), "head", None, None))
    return jax.shard_map(body, mesh=mesh, in_specs=in_specs, out_specs=out_specs, check_vma=False)
```
